128 devices in a mesh: front: 4 (over z_lo, core), grid: 32 (over z_hi, y, x).
Axes of the slice: x: 4, y: 4, z: 4 (z_hi: 2, z_lo: 2; z = z_hi * 2 + z_lo), core: 2. Of those that a mesh axis runs over, the one named last changes fastest.
Arguments:
- index_map: int32 [4, 8192], P('front'), may hold values from 0 to 16383, as said below
- lengths: int32 [4], P('front'), may hold values from 1 to 8192, 24576 in all
- update_front: float32 [4, 8192, 8192], P('front', 'grid'), may hold values from -0.0625 to 0.0625
- front_matrix: float32 [16384, 16384], P(('front', 'grid')), may hold values from -0.046875 to 0.046875
- random: float32 [16384, 256], P(('front', 'grid')), may hold values from -6 to 6
Outputs:
- parent_sample: float32 [16384, 256], P(('front', 'grid'))
The draws below stay inside these ranges and needn't reach their ends.
Inputs may be any that keep to these rules, and one draw needn't show every extreme that they name: `index_map`: within one child the 8192 entries are distinct parent rows. `lengths`: rows of a child at or past its length are not live; the largest length equals 8192.
All inputs are finite; a program needn't handle non-finite values. No bound on the sum of `lengths` on one device may be relied on, other than what follows from the above.
Results may differ from the reference program's by a relative error of at most 0.0003.
Values sent between devices are 32-bit elements; how exact they have to be, the bound alone decides.
No kernel may reach another device: no remote copies, remote signals or barrier semaphores. Data moves between devices by JAX's collectives and lax.ppermute only.
A program may use at most 128 MiB of HBM per device.

```python
import math
import jax
import jax.numpy as jnp
import numpy as np
from jax import lax

WP = 16384
UC = 8192
K = 256
CHILDREN = 4


def draw_index_map(key, part):
    child_keys = jax.random.split(jax.random.fold_in(key, 17), CHILDREN)
    picked = jax.vmap(lambda child_key: jax.random.permutation(child_key, WP)[:UC])(child_keys)
    return picked.astype(jnp.int32)


def levels(stream_key, shape, shards, smallest, largest):
    factor_of, own = 1.0, jax.random.fold_in(stream_key, 6)
    for position, shards_of in shards:
        heights = jnp.exp(jax.random.uniform(jax.random.fold_in(own, position), (shards_of,), jnp.float32, smallest / len(shards), largest / len(shards)))
        factor_of = factor_of * jnp.repeat(heights, shape[position] // shards_of).reshape([-1 if axis == position else 1 for axis in range(len(shape))])
    return factor_of


def length_profile(count, total, bound, skew):
    portions = [(1 << 20) // math.isqrt(standing ** skew) + 1 for standing in range(2, count + 1)]
    rest, holding = total - bound - (count - 1), [1] * (count - 1)
    while rest > 0:
        candidates = [i for i in range(count - 1) if holding[i] < bound]
        mass, remaining = sum([portions[i] for i in candidates]), rest
        for i in candidates:
            addition = min(bound - holding[i], max(1, remaining * portions[i] // mass), rest)
            holding[i] = holding[i] + addition
            rest = rest - addition
    return np.array([bound] + holding)


def ragged_sizes(stream_key, amount, total, reach, skew):
    if amount == 2:
        one = jax.random.randint(stream_key, (), max(1, total - reach), min(reach, total - 1) + 1)
        return jnp.stack([one, total - one])
    sizes = jnp.asarray(length_profile(amount, total, reach, skew), jnp.int32)
    twos = (amount - 1) // 2
    source_of, receiver = sizes[1:1 + 2 * twos:2], sizes[2:2 + 2 * twos:2]
    room = jnp.minimum(source_of - 1, reach - receiver)
    shifted = jax.random.randint(jax.random.fold_in(stream_key, 1), (twos,), 0, 1 << 20) % (room + 1)
    sizes = sizes.at[1:1 + 2 * twos:2].set(source_of - shifted).at[2:2 + 2 * twos:2].set(receiver + shifted)
    return sizes[jax.random.permutation(jax.random.fold_in(stream_key, 2), amount)]


def gaussian(key, dims, width, most, pieces=(), held_as=jnp.bfloat16):
    loudness = levels(key, dims, pieces, -0.22, 0.18) if pieces else 1.0
    drawn = jax.random.normal(key, dims, jnp.float32) * width * loudness
    return jnp.minimum(jnp.maximum(drawn, -most), most).astype(held_as)


def setup_inputs(seed: int = 0) -> dict:
    splits = jax.random.split(jax.random.key(seed), 6)
    return {
        "index_map": draw_index_map(jax.random.fold_in(splits[5], 71), 0),
        "lengths": ragged_sizes(splits[1], CHILDREN, 3 * UC, UC, 2).astype(jnp.int32),
        "update_front": gaussian(splits[2], (CHILDREN, UC, UC), UC ** -0.5, 0.0625, ((0, 4), (1, 32)), jnp.float32),
        "front_matrix": gaussian(splits[3], (WP, WP), WP ** -0.5, 0.046875, ((0, 128),), jnp.float32),
        "random": gaussian(splits[4], (WP, K), 1.0, 6.0, ((0, 128),), jnp.float32),
    }


def reference(index_map, lengths, update_front, front_matrix, random):
    parent_sample = jnp.dot(front_matrix, random, preferred_element_type=jnp.float32, precision=lax.Precision.HIGHEST)
    row_numbers = jnp.arange(UC, dtype=jnp.int32)

    def one_child(packed):
        child_rows, child_length, child_block = packed
        child_random = jnp.take(random, child_rows, axis=0)
        child_sample = jnp.dot(child_block, child_random, preferred_element_type=jnp.float32, precision=lax.Precision.HIGHEST)
        return jnp.where((row_numbers < child_length)[:, None], child_sample, jnp.float32(0.0))

    samples = lax.map(one_child, (index_map, lengths, update_front))
    for child in range(CHILDREN):
        parent_sample = parent_sample.at[index_map[child]].add(samples[child])
    return parent_sample
```

```python
import functools

import jax
import jax.numpy as jnp
import numpy as np
from jax import lax
from jax.experimental import pallas as pl
from jax.experimental.pallas import tpu as pltpu
from jax.sharding import PartitionSpec as P

AXES = ("front", "grid")
SIDE = 4


def places():
    return [
        (x, y, z_hi * 2 + z_lo, core)
        for z_lo in range(2)
        for core in range(2)
        for z_hi in range(2)
        for y in range(SIDE)
        for x in range(SIDE)
    ]


PLACES = places()
DEVICE = {place: i for i, place in enumerate(PLACES)}
BITS = [(z, y, x) for z in range(2) for y in range(2) for x in range(2)]


def cube_of(v, shift):
    return ((v - shift) % SIDE) // 2


def near_groups():
    groups = []
    for core in range(2):
        for cube in BITS:
            groups.append(
                [
                    DEVICE[tuple((2 * c + b + core) % SIDE for c, b in zip(cube[::-1], bit[::-1])) + (core,)]
                    for bit in BITS
                ]
            )
    return groups


def far_groups():
    groups = []
    for core in range(2):
        for cube in BITS:
            members = [DEVICE[tuple((2 * c + b + 1 - core) % SIDE for c, b in zip(cube[::-1], bit[::-1])) + (core,)] for bit in BITS]
            members.sort(key=lambda d: tuple(cube_of(PLACES[d][i], core) for i in (2, 1, 0)))
            groups.append(members)
    return groups


NEAR = near_groups()
FAR = far_groups()
CORES = [(i, DEVICE[(x, y, z, 1 - core)]) for i, (x, y, z, core) in enumerate(PLACES)]
LAYERS = [(i, DEVICE[(x, y, z ^ 1, core)]) for i, (x, y, z, core) in enumerate(PLACES)]


def map_rows():
    rows = np.zeros((len(PLACES), 16), np.int32)
    for group in NEAR:
        for d in group:
            for j, m in enumerate(group):
                x, y, z, _ = PLACES[m]
                for other in range(2):
                    layer = (z ^ PLACES[d][2]) & 1
                    rows[d, 2 * j + other] = (layer * 2 + other) * 32 + (z // 2) * 16 + y * 4 + x
    return rows


MAP_ROWS = map_rows()


def swap_cores(a):
    return lax.ppermute(a, AXES, CORES)


def spread(a, groups):
    copies = jnp.broadcast_to(a[None], (len(groups[0]), *a.shape))
    return lax.all_to_all(copies, AXES, 0, 0, tiled=True, axis_index_groups=groups)


def split2(a):
    high = a.astype(jnp.bfloat16)
    return high, (a - high.astype(jnp.float32)).astype(jnp.bfloat16)


def dot3(a, b):
    n = b.shape[1]
    a_high, a_low = split2(a)
    b_high, b_low = split2(b)
    both = jnp.dot(a_high, jnp.concatenate([b_high, b_low], axis=1), preferred_element_type=jnp.float32)
    return both[:, :n] + both[:, n:] + jnp.dot(a_low, b_high, preferred_element_type=jnp.float32)


def child_kernel(depth, own_at, other_at, random_ref, own_ref, other_ref, own_out, other_out, held, own_rows, other_rows, sem):
    step = pl.program_id(0)
    last = pl.num_programs(0) - 1
    place = lax.broadcasted_iota(jnp.int32, (8, 128), 0)

    def gather(at, chunk, rows):
        base = chunk * depth
        for j in range(0, depth, 8):
            tile = jnp.broadcast_to(held[pl.ds(at[base + j], 1), :], (8, 128))
            for t in range(1, 8):
                row = jnp.broadcast_to(held[pl.ds(at[base + j + t], 1), :], (8, 128))
                tile = jnp.where(place == t, row, tile)
            rows[j : j + 8, :] = tile

    @pl.when(step == 0)
    def _():
        copy = pltpu.make_async_copy(random_ref, held, sem)
        copy.start()
        copy.wait()
        own_out[...] = jnp.zeros_like(own_out)
        other_out[...] = jnp.zeros_like(other_out)
        gather(own_at, 0, own_rows.at[0])
        gather(other_at, 0, other_rows.at[0])

    slot = lax.rem(step, 2)
    later = jnp.minimum(step + 1, last)
    gather(own_at, later, own_rows.at[1 - slot])
    gather(other_at, later, other_rows.at[1 - slot])
    own_out[...] += dot3(own_ref[...], own_rows[slot])
    other_out[...] += dot3(other_ref[...], other_rows[slot])


def child_products(own_at, other_at, random, own, other, depth=1024):
    rows, inner = own.shape
    width = random.shape[1]
    out = jax.ShapeDtypeStruct((rows, width), jnp.float32)
    block = pl.BlockSpec((rows, depth), lambda k, *_: (0, k))
    whole = pl.BlockSpec((rows, width), lambda k, *_: (0, 0))
    return pl.pallas_call(
        functools.partial(child_kernel, depth),
        out_shape=(out, out),
        grid_spec=pltpu.PrefetchScalarGridSpec(
            num_scalar_prefetch=2,
            grid=(inner // depth,),
            in_specs=[pl.BlockSpec(memory_space=pl.ANY), block, block],
            out_specs=[whole, whole],
            scratch_shapes=[
                pltpu.VMEM(random.shape, jnp.float32),
                pltpu.VMEM((2, depth, width), jnp.float32),
                pltpu.VMEM((2, depth, width), jnp.float32),
                pltpu.SemaphoreType.DMA,
            ],
        ),
        compiler_params=pltpu.CompilerParams(vmem_limit_bytes=30 << 20),
        cost_estimate=pl.CostEstimate(flops=12 * rows * inner * width, bytes_accessed=24 << 20, transcendentals=0),
        name="child",
    )(own_at, other_at, random, own, other)


def front_kernel(depth, blocks, random_ref, own_ref, other_ref, out, held, sem):
    step = pl.program_id(0)

    @pl.when(step == 0)
    def _():
        copy = pltpu.make_async_copy(random_ref, held, sem)
        copy.start()
        copy.wait()
        out[...] = jnp.zeros_like(out)

    count = depth // 128
    rows = [held[pl.ds(pl.multiple_of(blocks[step * count + i] * 128, 128), 128), :] for i in range(count)]
    out[...] += dot3(jnp.concatenate([own_ref[...], other_ref[...]], axis=0), jnp.concatenate(rows, axis=0))


def front_products(blocks, random, own, other, depth=1024):
    rows, inner = own.shape
    width = random.shape[1]
    block = pl.BlockSpec((rows, depth), lambda k, *_: (0, k))
    return pl.pallas_call(
        functools.partial(front_kernel, depth),
        out_shape=jax.ShapeDtypeStruct((2 * rows, width), jnp.float32),
        grid_spec=pltpu.PrefetchScalarGridSpec(
            num_scalar_prefetch=1,
            grid=(inner // depth,),
            in_specs=[pl.BlockSpec(memory_space=pl.ANY), block, block],
            out_specs=pl.BlockSpec((2 * rows, width), lambda k, *_: (0, 0)),
            scratch_shapes=[pltpu.VMEM(random.shape, jnp.float32), pltpu.SemaphoreType.DMA],
        ),
        compiler_params=pltpu.CompilerParams(vmem_limit_bytes=30 << 20),
        cost_estimate=pl.CostEstimate(flops=12 * rows * inner * width, bytes_accessed=24 << 20, transcendentals=0),
        name="front",
    )(blocks, random, own, other)


def coordinates(block):
    front, grid = block >> 5, block & 31
    return grid & 3, (grid >> 2) & 3, (grid >> 4) * 2 + (front >> 1), front & 1


def held_block(block, core):
    x, y, z, owner = coordinates(block)
    x, y, z = (x - core) & 3, (y - core) & 3, (z - core) & 3
    far = (z >> 1) * 4 + (y >> 1) * 2 + (x >> 1)
    near = (z & 1) * 4 + (y & 1) * 2 + (x & 1)
    return (far * 8 + near) * 2 + (owner ^ core)


def shards(index_map, lengths, update_front, front_matrix, random):
    me = lax.axis_index("front") * 32 + lax.axis_index("grid")
    core = lax.axis_index("front") & 1
    width = random.shape[1] // 2
    own_rows = random.shape[0]
    sample_rows = update_front.shape[1]

    own_update, own_front = update_front[0], front_matrix
    left, right = random[:, :width], random[:, width:]
    kept = jnp.where(core == 0, left, right)
    given = jnp.where(core == 0, right, left)
    near = spread(jnp.concatenate([kept, swap_cores(given)], axis=0), NEAR)
    other_update = swap_cores(own_update)
    other_front = swap_cores(own_front)
    own_map = jnp.concatenate([index_map[0], jnp.broadcast_to(lengths, (128,))])
    maps = jnp.stack([own_map, swap_cores(own_map)])
    gathered = spread(near.reshape(-1, width), FAR).reshape(-1, width)

    live = maps[:, -1]
    maps = maps[:, :-128]
    at = held_block(maps >> 7, core) * 128 + (maps & 127)
    own_sample, other_sample = child_products(at[0], at[1], gathered, own_update, other_update)
    first = lax.axis_index("grid") * sample_rows
    rows = first + jnp.arange(sample_rows, dtype=jnp.int32)
    samples = jnp.where((rows[None, :] < live[:, None])[:, :, None], jnp.stack([own_sample, other_sample]), jnp.float32(0.0))
    cube = spread(samples, NEAR).reshape(-1, width)

    blocks = held_block(jnp.arange(WHOLE_BLOCKS, dtype=jnp.int32), core)
    front = front_products(blocks, gathered, own_front, other_front)

    layers = jnp.concatenate([maps, lax.ppermute(maps, AXES, LAYERS)]).reshape(-1, sample_rows)
    wanted = lax.dynamic_index_in_dim(jnp.asarray(MAP_ROWS), me, 0, keepdims=False)
    targets = jnp.take(layers, wanted, axis=0).reshape(-1)
    x, y, z, owner = coordinates(targets >> 7)
    grid = lax.axis_index("grid")
    mine = (grid & 3, (grid >> 2) & 3, (grid >> 4) * 2 + (lax.axis_index("front") >> 1))
    ours = functools.reduce(
        jnp.logical_and,
        [(((v - 1 + core) & 3) >> 1) == (((m - 1 + core) & 3) >> 1) for v, m in zip((x, y, z), mine)],
    )
    member = sum(((((v - core) & 3) >> 1) << i) for i, v in enumerate((x, y, z)))
    slots = jnp.where(ours, (member * 2 + (owner ^ core)) * own_rows + (targets & (own_rows - 1)), -1)
    chosen = (jnp.arange(16 * own_rows, dtype=jnp.int32)[:, None] == slots[None, :]).astype(jnp.bfloat16)
    rounded = lax.reduce_precision(cube, 8, 7)
    high, low = rounded.astype(jnp.bfloat16), (cube - rounded).astype(jnp.bfloat16)
    terms = jnp.dot(chosen, jnp.concatenate([high, low], axis=1), preferred_element_type=jnp.float32)
    terms = (terms[:, :width] + terms[:, width:]).reshape(8, 2 * own_rows, width)
    parts = lax.all_to_all(terms, AXES, 0, 0, tiled=True, axis_index_groups=FAR)
    total = front + jnp.sum(parts, axis=0)
    mine_half, other_half = total[:own_rows], swap_cores(total[own_rows:])
    return jnp.where(
        core == 0,
        jnp.concatenate([mine_half, other_half], axis=1),
        jnp.concatenate([other_half, mine_half], axis=1),
    )


WHOLE_BLOCKS = len(PLACES)


def solution(mesh):
    placed = (
        P("front", None),
        P("front"),
        P("front", "grid", None),
        P(("front", "grid"), None),
        P(("front", "grid"), None),
    )
    return jax.shard_map(
        shards, mesh=mesh, in_specs=placed, out_specs=P(("front", "grid"), None), check_vma=False
    )
```

```python
import functools

import jax
import jax.numpy as jnp
import numpy as np
from jax import lax
from jax.experimental import pallas as pl
from jax.experimental.pallas import tpu as pltpu
from jax.sharding import PartitionSpec as P

AXES = ("front", "grid")
SIDE = 4


def places():
    return [
        (x, y, z_hi * 2 + z_lo, core)
        for z_lo in range(2)
        for core in range(2)
        for z_hi in range(2)
        for y in range(SIDE)
        for x in range(SIDE)
    ]


PLACES = places()
DEVICE = {place: i for i, place in enumerate(PLACES)}
BITS = [(z, y, x) for z in range(2) for y in range(2) for x in range(2)]


def cube_of(v, shift):
    return ((v - shift) % SIDE) // 2


def near_groups():
    groups = []
    for core in range(2):
        for cube in BITS:
            groups.append(
                [
                    DEVICE[tuple((2 * c + b + core) % SIDE for c, b in zip(cube[::-1], bit[::-1])) + (core,)]
                    for bit in BITS
                ]
            )
    return groups


def far_groups():
    groups = []
    for core in range(2):
        for cube in BITS:
            members = [DEVICE[tuple((2 * c + b + 1 - core) % SIDE for c, b in zip(cube[::-1], bit[::-1])) + (core,)] for bit in BITS]
            members.sort(key=lambda d: tuple(cube_of(PLACES[d][i], core) for i in (2, 1, 0)))
            groups.append(members)
    return groups


NEAR = near_groups()
FAR = far_groups()
CORES = [(i, DEVICE[(x, y, z, 1 - core)]) for i, (x, y, z, core) in enumerate(PLACES)]
LAYERS = [(i, DEVICE[(x, y, z ^ 1, core)]) for i, (x, y, z, core) in enumerate(PLACES)]


def map_rows():
    rows = np.zeros((len(PLACES), 16), np.int32)
    for group in NEAR:
        for d in group:
            for j, m in enumerate(group):
                x, y, z, _ = PLACES[m]
                for other in range(2):
                    layer = (z ^ PLACES[d][2]) & 1
                    rows[d, 2 * j + other] = (layer * 2 + other) * 32 + (z // 2) * 16 + y * 4 + x
    return rows


MAP_ROWS = map_rows()


def swap_cores(a):
    return lax.ppermute(a, AXES, CORES)


def spread(a, groups):
    copies = jnp.broadcast_to(a[None], (len(groups[0]), *a.shape))
    return lax.all_to_all(copies, AXES, 0, 0, tiled=True, axis_index_groups=groups)


def halves(a):
    high = lax.reduce_precision(a, 8, 7)
    return high.astype(jnp.bfloat16), (a - high).astype(jnp.bfloat16)


def held_halves(rows):
    high = rows.astype(jnp.bfloat16)
    low = (rows - high.astype(jnp.float32)).astype(jnp.bfloat16)
    return high, low


def joined(p):
    m, n = p.shape[0] // 2, p.shape[1] // 2
    return (p[:m, :n] + p[m:, :n]) + (p[:m, n:] + p[m:, n:])


def child_kernel(depth, at, random, update, out, even, odd, fetched, sems):
    chunks = update.shape[1] // depth
    place = lax.broadcasted_iota(jnp.int32, (8, 128), 0)

    def fetch(chunk, slot):
        columns = pl.ds(pl.multiple_of(chunk * depth, depth), depth)
        return pltpu.make_async_copy(update.at[:, columns], fetched.at[slot], sems.at[slot])

    def gather(chunk, rows):
        base = chunk * depth
        for j in range(0, depth, 8):
            tile = jnp.broadcast_to(random[pl.ds(at[base + j], 1), :], (8, 128))
            for t in range(1, 8):
                row = jnp.broadcast_to(random[pl.ds(at[base + j + t], 1), :], (8, 128))
                tile = jnp.where(place == t, row, tile)
            rows[j : j + 8, :] = tile

    def product(slot, rows):
        stacked = jnp.concatenate(held_halves(fetched[slot]), axis=0)
        columns = jnp.concatenate(held_halves(rows[...]), axis=1)
        out[...] += joined(jnp.dot(stacked, columns, preferred_element_type=jnp.float32))

    fetch(0, 0).start()
    fetch(1, 1).start()
    gather(0, even)
    out[...] = jnp.zeros_like(out)

    def pair(i, carry):
        fetch(2 * i, 0).wait()
        gather(2 * i + 1, odd)
        product(0, even)

        @pl.when(2 * i + 2 < chunks)
        def _():
            fetch(2 * i + 2, 0).start()

        fetch(2 * i + 1, 1).wait()
        gather(jnp.minimum(2 * i + 2, chunks - 1), even)
        product(1, odd)

        @pl.when(2 * i + 3 < chunks)
        def _():
            fetch(2 * i + 3, 1).start()

        return carry

    lax.fori_loop(0, chunks // 2, pair, 0)


def child_product(at, random, update, limit, depth=1024):
    rows, inner = update.shape
    width = random.shape[1]
    whole = pl.BlockSpec(memory_space=pltpu.VMEM)
    return pl.pallas_call(
        functools.partial(child_kernel, depth),
        out_shape=jax.ShapeDtypeStruct((rows, width), jnp.float32),
        in_specs=[pl.BlockSpec(memory_space=pltpu.SMEM), whole, pl.BlockSpec(memory_space=pl.ANY)],
        out_specs=whole,
        scratch_shapes=[
            pltpu.VMEM((depth, width), jnp.float32),
            pltpu.VMEM((depth, width), jnp.float32),
            pltpu.VMEM((2, rows, depth), jnp.float32),
            pltpu.SemaphoreType.DMA((2,)),
        ],
        compiler_params=pltpu.CompilerParams(vmem_limit_bytes=limit),
        cost_estimate=pl.CostEstimate(flops=8 * rows * inner * width, bytes_accessed=16 << 20, transcendentals=0),
        name="child",
    )(at, random, update)


def front_kernel(depth, blocks, random, own, other, out):
    step = pl.program_id(0)
    count = depth // 128

    @pl.when(step == 0)
    def _():
        out[...] = jnp.zeros_like(out)

    rows = [random[pl.ds(pl.multiple_of(blocks[step * count + i] * 128, 128), 128), :] for i in range(count)]
    columns = jnp.concatenate(held_halves(jnp.concatenate(rows, axis=0)), axis=1)
    stacked = jnp.concatenate(held_halves(jnp.concatenate([own[...], other[...]], axis=0)), axis=0)
    out[...] += joined(jnp.dot(stacked, columns, preferred_element_type=jnp.float32))


def front_product(blocks, random, own, other, depth=2048):
    rows, inner = own.shape
    width = random.shape[1]
    block = pl.BlockSpec((rows, depth), lambda k, *_: (0, k))
    return pl.pallas_call(
        functools.partial(front_kernel, depth),
        out_shape=jax.ShapeDtypeStruct((2 * rows, width), jnp.float32),
        grid_spec=pltpu.PrefetchScalarGridSpec(
            num_scalar_prefetch=1,
            grid=(inner // depth,),
            in_specs=[pl.BlockSpec(random.shape, lambda k, *_: (0, 0), pipeline_mode=pl.Buffered(1)), block, block],
            out_specs=pl.BlockSpec((2 * rows, width), lambda k, *_: (0, 0)),
        ),
        compiler_params=pltpu.CompilerParams(vmem_limit_bytes=VMEM_LIMIT),
        cost_estimate=pl.CostEstimate(flops=16 * rows * inner * width, bytes_accessed=24 << 20, transcendentals=0),
        name="front",
    )(blocks, random, own, other)


def coordinates(block):
    front, grid = block >> 5, block & 31
    return grid & 3, (grid >> 2) & 3, (grid >> 4) * 2 + (front >> 1), front & 1


def held_block(block, core):
    x, y, z, owner = coordinates(block)
    x, y, z = (x - core) & 3, (y - core) & 3, (z - core) & 3
    far = (z >> 1) * 4 + (y >> 1) * 2 + (x >> 1)
    near = (z & 1) * 4 + (y & 1) * 2 + (x & 1)
    return (far * 8 + near) * 2 + (owner ^ core)


def shards(index_map, lengths, update_front, front_matrix, random):
    me = lax.axis_index("front") * 32 + lax.axis_index("grid")
    core = lax.axis_index("front") & 1
    width = random.shape[1] // 2
    own_rows = random.shape[0]
    sample_rows = update_front.shape[1]

    own_update, own_front = update_front[0], front_matrix
    left, right = random[:, :width], random[:, width:]
    kept = jnp.where(core == 0, left, right)
    given = jnp.where(core == 0, right, left)
    near = spread(jnp.concatenate([kept, swap_cores(given)], axis=0), NEAR)
    other_update = swap_cores(own_update)

    own_map = jnp.concatenate([index_map[0], jnp.broadcast_to(lengths, (128,))])
    maps = jnp.stack([own_map, swap_cores(own_map)])
    live = maps[:, -1]
    maps = maps[:, :-128]
    at = held_block(maps >> 7, core) * 128 + (maps & 127)
    own_at, other_at = at[0], at[1]
    first = lax.axis_index("grid") * sample_rows
    rows = first + jnp.arange(sample_rows, dtype=jnp.int32)
    own_live, other_live = rows < live[0], rows < live[1]
    blocks = held_block(jnp.arange(WHOLE_BLOCKS, dtype=jnp.int32), core)

    layers = jnp.concatenate([maps, lax.ppermute(maps, AXES, LAYERS)]).reshape(-1, sample_rows)
    wanted = lax.dynamic_index_in_dim(jnp.asarray(MAP_ROWS), me, 0, keepdims=False)
    targets = jnp.take(layers, wanted, axis=0)
    x, y, z, owner = coordinates(targets >> 7)
    grid = lax.axis_index("grid")
    mine = (grid & 3, (grid >> 2) & 3, (grid >> 4) * 2 + (lax.axis_index("front") >> 1))
    ours = functools.reduce(
        jnp.logical_and,
        [(((v - 1 + core) & 3) >> 1) == (((m - 1 + core) & 3) >> 1) for v, m in zip((x, y, z), mine)],
    )
    member = sum(((((v - core) & 3) >> 1) << i) for i, v in enumerate((x, y, z)))
    slots = jnp.where(ours, (member * 2 + (owner ^ core)) * own_rows + (targets & (own_rows - 1)), -1)
    own_slots, other_slots = slots[0::2].reshape(-1), slots[1::2].reshape(-1)

    near, other_update, own_at, other_at, own_live, other_live, blocks, own_slots, other_slots = lax.optimization_barrier(
        (near, other_update, own_at, other_at, own_live, other_live, blocks, own_slots, other_slots)
    )
    gathered = spread(near.reshape(-1, width), FAR).reshape(-1, width)
    gathered, given_front = lax.optimization_barrier((gathered, own_front))
    other_front = swap_cores(given_front)

    def masked(sample, alive):
        return jnp.where(alive[:, None], sample, jnp.float32(0.0))

    own_sample = child_product(own_at, gathered, own_update, SMALL_LIMIT)
    own_cube = spread(masked(own_sample, own_live), NEAR).reshape(-1, width)
    _, other_at = lax.optimization_barrier((own_sample, other_at))
    other_sample = child_product(other_at, gathered, other_update, VMEM_LIMIT)
    other_cube = spread(masked(other_sample, other_live), NEAR).reshape(-1, width)
    own_cube, _, blocks = lax.optimization_barrier((own_cube, other_sample, blocks))
    front = front_product(blocks, gathered, own_front, other_front)

    def placed(cube, at_slots):
        chosen = (jnp.arange(16 * own_rows, dtype=jnp.int32)[:, None] == at_slots[None, :]).astype(jnp.bfloat16)
        terms = jnp.dot(chosen, jnp.concatenate(halves(cube), axis=1), preferred_element_type=jnp.float32)
        return terms[:, :width] + terms[:, width:]

    own_terms = placed(own_cube, own_slots)
    _, other_cube, front = lax.optimization_barrier((own_terms, other_cube, front))
    terms = own_terms + placed(other_cube, other_slots)
    parts = lax.all_to_all(terms.reshape(8, 2 * own_rows, width), AXES, 0, 0, tiled=True, axis_index_groups=FAR)
    total = front + jnp.sum(parts, axis=0)
    mine_half, other_half = total[:own_rows], swap_cores(total[own_rows:])
    return jnp.where(
        core == 0,
        jnp.concatenate([mine_half, other_half], axis=1),
        jnp.concatenate([other_half, mine_half], axis=1),
    )


VMEM_LIMIT = 48 << 20
SMALL_LIMIT = 32 << 20
WHOLE_BLOCKS = len(PLACES)


def solution(mesh):
    placed = (
        P("front", None),
        P("front"),
        P("front", "grid", None),
        P(("front", "grid"), None),
        P(("front", "grid"), None),
    )
    return jax.shard_map(
        shards, mesh=mesh, in_specs=placed, out_specs=P(("front", "grid"), None), check_vma=False
    )
```

```python
import functools

import jax
import jax.numpy as jnp
import numpy as np
from jax import lax
from jax.experimental import pallas as pl
from jax.experimental.pallas import tpu as pltpu
from jax.sharding import PartitionSpec as P

AXES = ("front", "grid")
SIDE = 4


def places():
    return [
        (x, y, z_hi * 2 + z_lo, core)
        for z_lo in range(2)
        for core in range(2)
        for z_hi in range(2)
        for y in range(SIDE)
        for x in range(SIDE)
    ]


PLACES = places()
DEVICE = {place: i for i, place in enumerate(PLACES)}
BITS = [(z, y, x) for z in range(2) for y in range(2) for x in range(2)]


def cube_of(v, shift):
    return ((v - shift) % SIDE) // 2


def near_groups():
    groups = []
    for core in range(2):
        for cube in BITS:
            groups.append(
                [
                    DEVICE[tuple((2 * c + b + core) % SIDE for c, b in zip(cube[::-1], bit[::-1])) + (core,)]
                    for bit in BITS
                ]
            )
    return groups


def far_groups():
    groups = []
    for core in range(2):
        for cube in BITS:
            members = [DEVICE[tuple((2 * c + b + 1 - core) % SIDE for c, b in zip(cube[::-1], bit[::-1])) + (core,)] for bit in BITS]
            members.sort(key=lambda d: tuple(cube_of(PLACES[d][i], core) for i in (2, 1, 0)))
            groups.append(members)
    return groups


NEAR = near_groups()
FAR = far_groups()
CORES = [(i, DEVICE[(x, y, z, 1 - core)]) for i, (x, y, z, core) in enumerate(PLACES)]
BOTH = [(i, DEVICE[(x, y, z ^ 1, 1 - core)]) for i, (x, y, z, core) in enumerate(PLACES)]
LAYERS = [(i, DEVICE[(x, y, z ^ 1, core)]) for i, (x, y, z, core) in enumerate(PLACES)]


def map_rows():
    rows = np.zeros((len(PLACES), 16), np.int32)
    for group in NEAR:
        for d in group:
            for j, m in enumerate(group):
                x, y, z, _ = PLACES[m]
                for other in range(2):
                    layer = (z ^ PLACES[d][2]) & 1
                    rows[d, 2 * j + other] = (layer * 2 + other) * 32 + (z // 2) * 16 + y * 4 + x
    return rows


MAP_ROWS = map_rows()


def swap_cores(a):
    return lax.ppermute(a, AXES, CORES)


def spread(a, groups):
    copies = jnp.broadcast_to(a[None], (len(groups[0]), *a.shape))
    return lax.all_to_all(copies, AXES, 0, 0, tiled=True, axis_index_groups=groups)


def halves(a):
    high = lax.reduce_precision(a, 8, 7)
    return high.astype(jnp.bfloat16), (a - high).astype(jnp.bfloat16)


def held_halves(rows):
    high = rows.astype(jnp.bfloat16)
    low = (rows - high.astype(jnp.float32)).astype(jnp.bfloat16)
    return high, low


def joined(p):
    m, n = p.shape[0] // 2, p.shape[1] // 2
    return (p[:m, :n] + p[m:, :n]) + (p[:m, n:] + p[m:, n:])


def child_kernel(depth, own_at, other_at, random, own, other, own_out, other_out, even, odd, own_held, other_held, sems):
    chunks = own.shape[1] // depth
    place = lax.broadcasted_iota(jnp.int32, (8, 128), 0)

    def fetch(chunk, update, held, sem):
        columns = pl.ds(pl.multiple_of(chunk * depth, depth), depth)
        return pltpu.make_async_copy(update.at[:, columns], held, sem)

    def gather(at, chunk, rows):
        base = chunk * depth
        for j in range(0, depth, 8):
            tile = jnp.broadcast_to(random[pl.ds(at[base + j], 1), :], (8, 128))
            for t in range(1, 8):
                row = jnp.broadcast_to(random[pl.ds(at[base + j + t], 1), :], (8, 128))
                tile = jnp.where(place == t, row, tile)
            rows[j : j + 8, :] = tile

    def product(held, rows, out):
        stacked = jnp.concatenate(held_halves(held[...]), axis=0)
        columns = jnp.concatenate(held_halves(rows[...]), axis=1)
        out[...] += joined(jnp.dot(stacked, columns, preferred_element_type=jnp.float32))

    fetch(0, own, own_held, sems.at[0]).start()
    fetch(0, other, other_held, sems.at[1]).start()
    gather(own_at, 0, even)
    own_out[...] = jnp.zeros_like(own_out)
    other_out[...] = jnp.zeros_like(other_out)

    def step(i, carry):
        fetch(i, own, own_held, sems.at[0]).wait()
        gather(other_at, i, odd)
        product(own_held, even, own_out)

        @pl.when(i + 1 < chunks)
        def _():
            fetch(i + 1, own, own_held, sems.at[0]).start()

        fetch(i, other, other_held, sems.at[1]).wait()
        gather(own_at, jnp.minimum(i + 1, chunks - 1), even)
        product(other_held, odd, other_out)

        @pl.when(i + 1 < chunks)
        def _():
            fetch(i + 1, other, other_held, sems.at[1]).start()

        return carry

    lax.fori_loop(0, chunks, step, 0)


def child_products(own_at, other_at, random, own, other, depth=1024):
    rows, inner = own.shape
    width = random.shape[1]
    whole = pl.BlockSpec(memory_space=pltpu.VMEM)
    anywhere = pl.BlockSpec(memory_space=pl.ANY)
    index = pl.BlockSpec(memory_space=pltpu.SMEM)
    out = jax.ShapeDtypeStruct((rows, width), jnp.float32)
    return pl.pallas_call(
        functools.partial(child_kernel, depth),
        out_shape=(out, out),
        in_specs=[index, index, whole, anywhere, anywhere],
        out_specs=(whole, whole),
        scratch_shapes=[
            pltpu.VMEM((depth, width), jnp.float32),
            pltpu.VMEM((depth, width), jnp.float32),
            pltpu.VMEM((rows, depth), jnp.float32),
            pltpu.VMEM((rows, depth), jnp.float32),
            pltpu.SemaphoreType.DMA((2,)),
        ],
        compiler_params=pltpu.CompilerParams(vmem_limit_bytes=SMALL_LIMIT),
        cost_estimate=pl.CostEstimate(flops=16 * rows * inner * width, bytes_accessed=24 << 20, transcendentals=0),
        name="child",
    )(own_at, other_at, random, own, other)


def front_kernel(depth, blocks, random, own, other, out):
    step = pl.program_id(0)
    count = depth // 128

    @pl.when(step == 0)
    def _():
        out[...] = jnp.zeros_like(out)

    rows = [random[pl.ds(pl.multiple_of(blocks[step * count + i] * 128, 128), 128), :] for i in range(count)]
    columns = jnp.concatenate(held_halves(jnp.concatenate(rows, axis=0)), axis=1)
    stacked = jnp.concatenate(held_halves(jnp.concatenate([own[...], other[...]], axis=0)), axis=0)
    out[...] += joined(jnp.dot(stacked, columns, preferred_element_type=jnp.float32))


def front_product(blocks, random, own, other, depth=2048):
    rows, inner = own.shape
    width = random.shape[1]
    block = pl.BlockSpec((rows, depth), lambda k, *_: (0, k))
    return pl.pallas_call(
        functools.partial(front_kernel, depth),
        out_shape=jax.ShapeDtypeStruct((2 * rows, width), jnp.float32),
        grid_spec=pltpu.PrefetchScalarGridSpec(
            num_scalar_prefetch=1,
            grid=(inner // depth,),
            in_specs=[pl.BlockSpec(random.shape, lambda k, *_: (0, 0), pipeline_mode=pl.Buffered(1)), block, block],
            out_specs=pl.BlockSpec((2 * rows, width), lambda k, *_: (0, 0)),
        ),
        compiler_params=pltpu.CompilerParams(vmem_limit_bytes=VMEM_LIMIT),
        cost_estimate=pl.CostEstimate(flops=16 * rows * inner * width, bytes_accessed=24 << 20, transcendentals=0),
        name="front",
    )(blocks, random, own, other)


def coordinates(block):
    front, grid = block >> 5, block & 31
    return grid & 3, (grid >> 2) & 3, (grid >> 4) * 2 + (front >> 1), front & 1


def held_block(block, core):
    x, y, z, owner = coordinates(block)
    x, y, z = (x - core) & 3, (y - core) & 3, (z - core) & 3
    far = (z >> 1) * 4 + (y >> 1) * 2 + (x >> 1)
    near = (z & 1) * 4 + (y & 1) * 2 + (x & 1)
    return (far * 8 + near) * 2 + (owner ^ core)


def shards(index_map, lengths, update_front, front_matrix, random):
    me = lax.axis_index("front") * 32 + lax.axis_index("grid")
    core = lax.axis_index("front") & 1
    width = random.shape[1] // 2
    own_rows = random.shape[0]
    sample_rows = update_front.shape[1]

    own_update, own_front = update_front[0], front_matrix
    left, right = random[:, :width], random[:, width:]
    kept = jnp.where(core == 0, left, right)
    given = jnp.where(core == 0, right, left)
    halved = jnp.concatenate([kept, swap_cores(given)], axis=0)
    near = spread(halved, NEAR)

    own_map = jnp.concatenate([index_map[0], jnp.broadcast_to(lengths, (128,))])
    next_maps = [lax.ppermute(own_map, AXES, pairs) for pairs in (CORES, LAYERS, BOTH)]
    _, given_update, all_maps = lax.optimization_barrier((halved, own_update, (own_map, *next_maps)))
    other_update = swap_cores(given_update)

    all_maps = jnp.stack(all_maps)
    live = all_maps[:2, -1]
    all_maps = all_maps[:, :-128]
    maps = all_maps[:2]
    at = held_block(maps >> 7, core) * 128 + (maps & 127)
    own_at, other_at = at[0], at[1]
    first = lax.axis_index("grid") * sample_rows
    rows = first + jnp.arange(sample_rows, dtype=jnp.int32)
    alive = rows[None, :] < live[:, None]
    blocks = held_block(jnp.arange(WHOLE_BLOCKS, dtype=jnp.int32), core)

    layers = all_maps.reshape(-1, sample_rows)
    wanted = lax.dynamic_index_in_dim(jnp.asarray(MAP_ROWS), me, 0, keepdims=False)
    targets = jnp.take(layers, wanted, axis=0)
    x, y, z, owner = coordinates(targets >> 7)
    grid = lax.axis_index("grid")
    mine = (grid & 3, (grid >> 2) & 3, (grid >> 4) * 2 + (lax.axis_index("front") >> 1))
    ours = functools.reduce(
        jnp.logical_and,
        [(((v - 1 + core) & 3) >> 1) == (((m - 1 + core) & 3) >> 1) for v, m in zip((x, y, z), mine)],
    )
    member = sum(((((v - core) & 3) >> 1) << i) for i, v in enumerate((x, y, z)))
    slots = jnp.where(ours, (member * 2 + (owner ^ core)) * own_rows + (targets & (own_rows - 1)), -1)
    slots = slots.reshape(-1)

    near, other_update, own_at, other_at, alive, blocks, slots = lax.optimization_barrier(
        (near, other_update, own_at, other_at, alive, blocks, slots)
    )
    gathered = spread(near.reshape(-1, width), FAR).reshape(-1, width)
    gathered, given_front = lax.optimization_barrier((gathered, own_front))
    other_front = swap_cores(given_front)

    samples = jnp.stack(child_products(own_at, other_at, gathered, own_update, other_update))
    samples = jnp.where(alive[:, :, None], samples, jnp.float32(0.0))
    cube = spread(samples, NEAR).reshape(-1, width)
    _, blocks = lax.optimization_barrier((samples, blocks))
    front = front_product(blocks, gathered, own_front, other_front)

    cube, front = lax.optimization_barrier((cube, front))
    chosen = (jnp.arange(16 * own_rows, dtype=jnp.int32)[:, None] == slots[None, :]).astype(jnp.bfloat16)
    terms = jnp.dot(chosen, jnp.concatenate(halves(cube), axis=1), preferred_element_type=jnp.float32)
    terms = terms[:, :width] + terms[:, width:]
    parts = lax.all_to_all(terms.reshape(8, 2 * own_rows, width), AXES, 0, 0, tiled=True, axis_index_groups=FAR)
    total = front + jnp.sum(parts, axis=0)
    mine_half, other_half = total[:own_rows], swap_cores(total[own_rows:])
    return jnp.where(
        core == 0,
        jnp.concatenate([mine_half, other_half], axis=1),
        jnp.concatenate([other_half, mine_half], axis=1),
    )


VMEM_LIMIT = 48 << 20
SMALL_LIMIT = 32 << 20
WHOLE_BLOCKS = len(PLACES)


def solution(mesh):
    placed = (
        P("front", None),
        P("front"),
        P("front", "grid", None),
        P(("front", "grid"), None),
        P(("front", "grid"), None),
    )
    return jax.shard_map(
        shards, mesh=mesh, in_specs=placed, out_specs=P(("front", "grid"), None), check_vma=False
    )
```

```python
import functools

import jax
import jax.numpy as jnp
import numpy as np
from jax import lax
from jax.experimental import pallas as pl
from jax.experimental.pallas import tpu as pltpu
from jax.sharding import PartitionSpec as P

AXES = ("front", "grid")
SIDE = 4


def places():
    return [
        (x, y, z_hi * 2 + z_lo, core)
        for z_lo in range(2)
        for core in range(2)
        for z_hi in range(2)
        for y in range(SIDE)
        for x in range(SIDE)
    ]


PLACES = places()
DEVICE = {place: i for i, place in enumerate(PLACES)}
BITS = [(z, y, x) for z in range(2) for y in range(2) for x in range(2)]


def near_groups():
    groups = []
    for core in range(2):
        for cube in BITS:
            groups.append(
                [
                    DEVICE[tuple((2 * c + b + core) % SIDE for c, b in zip(cube[::-1], bit[::-1])) + (core,)]
                    for bit in BITS
                ]
            )
    return groups


def far_groups():
    groups = []
    for core in range(2):
        for cube in BITS:
            groups.append(
                [
                    DEVICE[tuple((2 * c + b + 1 - core) % SIDE for c, b in zip(cube[::-1], bit[::-1])) + (core,)]
                    for bit in BITS
                ]
            )
    return groups


NEAR = near_groups()
FAR = far_groups()
CORES = [(i, DEVICE[(x, y, z, 1 - core)]) for i, (x, y, z, core) in enumerate(PLACES)]
LAYERS = [(i, DEVICE[(x, y, z ^ 1, core)]) for i, (x, y, z, core) in enumerate(PLACES)]


def map_rows():
    rows = np.zeros((len(PLACES), 16), np.int32)
    for group in NEAR:
        for d in group:
            for j, m in enumerate(group):
                x, y, z, _ = PLACES[m]
                for other in range(2):
                    layer = (z ^ PLACES[d][2]) & 1
                    rows[d, 2 * j + other] = (layer * 2 + other) * 32 + (z // 2) * 16 + y * 4 + x
    return rows


MAP_ROWS = map_rows()


def swap_cores(a):
    return lax.ppermute(a, AXES, CORES)


def spread(a, groups):
    copies = jnp.broadcast_to(a[None], (len(groups[0]), *a.shape))
    return lax.all_to_all(copies, AXES, 0, 0, tiled=True, axis_index_groups=groups)


def halves(a):
    high = lax.reduce_precision(a, 8, 7)
    return high.astype(jnp.bfloat16), (a - high).astype(jnp.bfloat16)


def held_halves(rows):
    high = rows.astype(jnp.bfloat16)
    low = (rows - high.astype(jnp.float32)).astype(jnp.bfloat16)
    return high, low


def joined(p):
    m, n = p.shape[0] // 2, p.shape[1] // 2
    return (p[:m, :n] + p[m:, :n]) + (p[:m, n:] + p[m:, n:])


def child_kernel(depth, own_at, other_at, random, own, other, own_out, other_out, even, odd, own_held, other_held, sems):
    chunks = own.shape[1] // depth
    place = lax.broadcasted_iota(jnp.int32, (8, 128), 0)

    def fetch(chunk, update, held, sem):
        columns = pl.ds(pl.multiple_of(chunk * depth, depth), depth)
        return pltpu.make_async_copy(update.at[:, columns], held, sem)

    def gather(at, chunk, rows):
        base = chunk * depth
        for j in range(0, depth, 8):
            tile = jnp.broadcast_to(random[pl.ds(at[base + j], 1), :], (8, 128))
            for t in range(1, 8):
                row = jnp.broadcast_to(random[pl.ds(at[base + j + t], 1), :], (8, 128))
                tile = jnp.where(place == t, row, tile)
            rows[j : j + 8, :] = tile

    def product(held, rows, out):
        stacked = jnp.concatenate(held_halves(held[...]), axis=0)
        columns = jnp.concatenate(held_halves(rows[...]), axis=1)
        out[...] += joined(jnp.dot(stacked, columns, preferred_element_type=jnp.float32))

    fetch(0, own, own_held, sems.at[0]).start()
    fetch(0, other, other_held, sems.at[1]).start()
    gather(own_at, 0, even)
    own_out[...] = jnp.zeros_like(own_out)
    other_out[...] = jnp.zeros_like(other_out)

    def step(i, carry):
        fetch(i, own, own_held, sems.at[0]).wait()
        gather(other_at, i, odd)
        product(own_held, even, own_out)

        @pl.when(i + 1 < chunks)
        def _():
            fetch(i + 1, own, own_held, sems.at[0]).start()

        fetch(i, other, other_held, sems.at[1]).wait()
        gather(own_at, jnp.minimum(i + 1, chunks - 1), even)
        product(other_held, odd, other_out)

        @pl.when(i + 1 < chunks)
        def _():
            fetch(i + 1, other, other_held, sems.at[1]).start()

        return carry

    lax.fori_loop(0, chunks, step, 0)


def child_products(own_at, other_at, random, own, other, depth=2048):
    rows, inner = own.shape
    width = random.shape[1]
    whole = pl.BlockSpec(memory_space=pltpu.VMEM)
    anywhere = pl.BlockSpec(memory_space=pl.ANY)
    index = pl.BlockSpec(memory_space=pltpu.SMEM)
    out = jax.ShapeDtypeStruct((rows, width), jnp.float32)
    return pl.pallas_call(
        functools.partial(child_kernel, depth),
        out_shape=(out, out),
        in_specs=[index, index, whole, anywhere, anywhere],
        out_specs=(whole, whole),
        scratch_shapes=[
            pltpu.VMEM((depth, width), jnp.float32),
            pltpu.VMEM((depth, width), jnp.float32),
            pltpu.VMEM((rows, depth), jnp.float32),
            pltpu.VMEM((rows, depth), jnp.float32),
            pltpu.SemaphoreType.DMA((2,)),
        ],
        compiler_params=pltpu.CompilerParams(vmem_limit_bytes=SMALL_LIMIT),
        cost_estimate=pl.CostEstimate(flops=16 * rows * inner * width, bytes_accessed=24 << 20, transcendentals=0),
        name="child",
    )(own_at, other_at, random, own, other)


def front_kernel(depth, blocks, random, own, other, out):
    step = pl.program_id(0)
    count = depth // 128

    @pl.when(step == 0)
    def _():
        out[...] = jnp.zeros_like(out)

    rows = [random[pl.ds(pl.multiple_of(blocks[step * count + i] * 128, 128), 128), :] for i in range(count)]
    columns = jnp.concatenate(held_halves(jnp.concatenate(rows, axis=0)), axis=1)
    stacked = jnp.concatenate(held_halves(jnp.concatenate([own[...], other[...]], axis=0)), axis=0)
    out[...] += joined(jnp.dot(stacked, columns, preferred_element_type=jnp.float32))


def front_product(blocks, random, own, other, depth=4096):
    rows, inner = own.shape
    width = random.shape[1]
    block = pl.BlockSpec((rows, depth), lambda k, *_: (0, k))
    return pl.pallas_call(
        functools.partial(front_kernel, depth),
        out_shape=jax.ShapeDtypeStruct((2 * rows, width), jnp.float32),
        grid_spec=pltpu.PrefetchScalarGridSpec(
            num_scalar_prefetch=1,
            grid=(inner // depth,),
            in_specs=[pl.BlockSpec(random.shape, lambda k, *_: (0, 0), pipeline_mode=pl.Buffered(1)), block, block],
            out_specs=pl.BlockSpec((2 * rows, width), lambda k, *_: (0, 0)),
        ),
        compiler_params=pltpu.CompilerParams(vmem_limit_bytes=VMEM_LIMIT),
        cost_estimate=pl.CostEstimate(flops=16 * rows * inner * width, bytes_accessed=24 << 20, transcendentals=0),
        name="front",
    )(blocks, random, own, other)


def coordinates(block):
    front, grid = block >> 5, block & 31
    return grid & 3, (grid >> 2) & 3, (grid >> 4) * 2 + (front >> 1), front & 1


def far_cube(v, core):
    return ((v - 1 + core) & 3) >> 1


def held_block(block, here, core):
    *there, owner = coordinates(block)
    far = near = 0
    for i, (v, m) in enumerate(zip(there, here)):
        v = (v - core) & 3
        far += ((v >> 1) ^ far_cube(m, core) ^ core) << i
        near += (v & 1) << i
    return (far * 8 + near) * 2 + (owner ^ core)


def shards(index_map, lengths, update_front, front_matrix, random):
    me = lax.axis_index("front") * 32 + lax.axis_index("grid")
    core = lax.axis_index("front") & 1
    width = random.shape[1] // 2
    own_rows = random.shape[0]
    grid = lax.axis_index("grid")
    here = (grid & 3, (grid >> 2) & 3, (grid >> 4) * 2 + (lax.axis_index("front") >> 1))
    sample_rows = update_front.shape[1]

    own_update, own_front = update_front[0], front_matrix
    left, right = random[:, :width], random[:, width:]
    kept = jnp.where(core == 0, left, right)
    given = jnp.where(core == 0, right, left)
    halved = jnp.concatenate([kept, swap_cores(given)], axis=0)
    near = spread(halved, NEAR)

    own_map = jnp.concatenate([index_map[0], jnp.broadcast_to(lengths, (128,))])
    other_map = swap_cores(own_map)
    _, _, given_update = lax.optimization_barrier((halved, other_map, own_update))
    other_update = swap_cores(given_update)

    maps = jnp.stack([own_map, other_map])
    live = maps[:, -1]
    maps = maps[:, :-128]
    at = held_block(maps >> 7, here, core) * 128 + (maps & 127)
    own_at, other_at = at[0], at[1]
    first = grid * sample_rows
    rows = first + jnp.arange(sample_rows, dtype=jnp.int32)
    alive = rows[None, :] < live[:, None]
    blocks = held_block(jnp.arange(WHOLE_BLOCKS, dtype=jnp.int32), here, core)

    near, other_update, own_at, other_at, alive, blocks = lax.optimization_barrier(
        (near, other_update, own_at, other_at, alive, blocks)
    )
    gathered = spread(near.reshape(-1, width), FAR).reshape(-1, width)
    gathered, given_front = lax.optimization_barrier((gathered, own_front))
    other_front = swap_cores(given_front)

    samples = jnp.stack(child_products(own_at, other_at, gathered, own_update, other_update))
    samples = jnp.where(alive[:, :, None], samples, jnp.float32(0.0))
    cube = spread(samples, NEAR).reshape(-1, width)
    _, blocks, maps, here = lax.optimization_barrier((samples, blocks, maps, here))
    front = front_product(blocks, gathered, own_front, other_front)

    layers = jnp.concatenate([maps, lax.ppermute(maps, AXES, LAYERS)]).reshape(-1, sample_rows)
    wanted = lax.dynamic_index_in_dim(jnp.asarray(MAP_ROWS), me, 0, keepdims=False)
    targets = layers.at[wanted].get(mode="promise_in_bounds")
    *there, owner = coordinates(targets >> 7)
    ours = functools.reduce(jnp.logical_and, [far_cube(v, core) == far_cube(m, core) for v, m in zip(there, here)])
    member = sum(((v - 1 + core) & 1) << i for i, v in enumerate(there))
    slots = jnp.where(ours, (member * 2 + (owner ^ core)) * own_rows + (targets & (own_rows - 1)), -1)
    slots = slots.reshape(-1)

    cube, front = lax.optimization_barrier((cube, front))
    chosen = (jnp.arange(16 * own_rows, dtype=jnp.int32)[:, None] == slots[None, :]).astype(jnp.bfloat16)
    terms = jnp.dot(chosen, jnp.concatenate(halves(cube), axis=1), preferred_element_type=jnp.float32)
    terms = terms[:, :width] + terms[:, width:]
    parts = lax.all_to_all(terms.reshape(8, 2 * own_rows, width), AXES, 0, 0, tiled=True, axis_index_groups=FAR)
    total = front + jnp.sum(parts, axis=0)
    mine_half, other_half = total[:own_rows], swap_cores(total[own_rows:])
    return jnp.where(
        core == 0,
        jnp.concatenate([mine_half, other_half], axis=1),
        jnp.concatenate([other_half, mine_half], axis=1),
    )


VMEM_LIMIT = 48 << 20
SMALL_LIMIT = 32 << 20
WHOLE_BLOCKS = len(PLACES)


def solution(mesh):
    placed = (
        P("front", None),
        P("front"),
        P("front", "grid", None),
        P(("front", "grid"), None),
        P(("front", "grid"), None),
    )
    return jax.shard_map(
        shards, mesh=mesh, in_specs=placed, out_specs=P(("front", "grid"), None), check_vma=False
    )
```

```python
import functools

import jax
import jax.numpy as jnp
import numpy as np
from jax import lax
from jax.experimental import pallas as pl
from jax.experimental.pallas import tpu as pltpu
from jax.sharding import PartitionSpec as P

AXES = ("front", "grid")
SIDE = 4


def places():
    return [
        (x, y, z_hi * 2 + z_lo, core)
        for z_lo in range(2)
        for core in range(2)
        for z_hi in range(2)
        for y in range(SIDE)
        for x in range(SIDE)
    ]


PLACES = places()
DEVICE = {place: i for i, place in enumerate(PLACES)}
BITS = [(z, y, x) for z in range(2) for y in range(2) for x in range(2)]


def near_groups():
    groups = []
    for core in range(2):
        for cube in BITS:
            groups.append(
                [
                    DEVICE[tuple((2 * c + b + core) % SIDE for c, b in zip(cube[::-1], bit[::-1])) + (core,)]
                    for bit in BITS
                ]
            )
    return groups


def far_groups():
    groups = []
    for core in range(2):
        for cube in BITS:
            groups.append(
                [
                    DEVICE[tuple((2 * c + b + 1 - core) % SIDE for c, b in zip(cube[::-1], bit[::-1])) + (core,)]
                    for bit in BITS
                ]
            )
    return groups


NEAR = near_groups()
FAR = far_groups()
CORES = [(i, DEVICE[(x, y, z, 1 - core)]) for i, (x, y, z, core) in enumerate(PLACES)]
LAYERS = [(i, DEVICE[(x, y, z ^ 1, core)]) for i, (x, y, z, core) in enumerate(PLACES)]


def map_rows():
    rows = np.zeros((len(PLACES), 16), np.int32)
    for group in NEAR:
        for d in group:
            for j, m in enumerate(group):
                x, y, z, _ = PLACES[m]
                for other in range(2):
                    layer = (z ^ PLACES[d][2]) & 1
                    rows[d, 2 * j + other] = (layer * 2 + other) * 32 + (z // 2) * 16 + y * 4 + x
    return rows


MAP_ROWS = map_rows()


def swap_cores(a):
    return lax.ppermute(a, AXES, CORES)


def spread(a, groups):
    copies = jnp.broadcast_to(a[None], (len(groups[0]), *a.shape))
    return lax.all_to_all(copies, AXES, 0, 0, tiled=True, axis_index_groups=groups)


def halves(a):
    high = lax.reduce_precision(a, 8, 7)
    return high.astype(jnp.bfloat16), (a - high).astype(jnp.bfloat16)


def held_halves(rows):
    high = rows.astype(jnp.bfloat16)
    low = (rows - high.astype(jnp.float32)).astype(jnp.bfloat16)
    return high, low


def joined(p):
    m, n = p.shape[0] // 2, p.shape[1] // 2
    return (p[:m, :n] + p[m:, :n]) + (p[:m, n:] + p[m:, n:])


def child_kernel(depth, own_at, other_at, random, own, other, own_out, other_out, even, odd, own_held, other_held, sems):
    chunks = own.shape[1] // depth
    place = lax.broadcasted_iota(jnp.int32, (8, 128), 0)

    def fetch(chunk, update, held, sem):
        columns = pl.ds(pl.multiple_of(chunk * depth, depth), depth)
        return pltpu.make_async_copy(update.at[:, columns], held, sem)

    def gather(at, chunk, rows):
        base = chunk * depth
        for j in range(0, depth, 8):
            tile = jnp.broadcast_to(random[pl.ds(at[base + j], 1), :], (8, 128))
            for t in range(1, 8):
                row = jnp.broadcast_to(random[pl.ds(at[base + j + t], 1), :], (8, 128))
                tile = jnp.where(place == t, row, tile)
            rows[j : j + 8, :] = tile

    def product(held, rows, out):
        stacked = jnp.concatenate(held_halves(held[...]), axis=0)
        columns = jnp.concatenate(held_halves(rows[...]), axis=1)
        out[...] += joined(jnp.dot(stacked, columns, preferred_element_type=jnp.float32))

    fetch(0, own, own_held, sems.at[0]).start()
    fetch(0, other, other_held, sems.at[1]).start()
    gather(own_at, 0, even)
    own_out[...] = jnp.zeros_like(own_out)
    other_out[...] = jnp.zeros_like(other_out)

    def step(i, carry):
        fetch(i, own, own_held, sems.at[0]).wait()
        gather(other_at, i, odd)
        product(own_held, even, own_out)

        @pl.when(i + 1 < chunks)
        def _():
            fetch(i + 1, own, own_held, sems.at[0]).start()

        fetch(i, other, other_held, sems.at[1]).wait()
        gather(own_at, jnp.minimum(i + 1, chunks - 1), even)
        product(other_held, odd, other_out)

        @pl.when(i + 1 < chunks)
        def _():
            fetch(i + 1, other, other_held, sems.at[1]).start()

        return carry

    lax.fori_loop(0, chunks, step, 0)


def child_products(own_at, other_at, random, own, other, depth=2048):
    rows, inner = own.shape
    width = random.shape[1]
    whole = pl.BlockSpec(memory_space=pltpu.VMEM)
    anywhere = pl.BlockSpec(memory_space=pl.ANY)
    index = pl.BlockSpec(memory_space=pltpu.SMEM)
    out = jax.ShapeDtypeStruct((rows, width), jnp.float32)
    return pl.pallas_call(
        functools.partial(child_kernel, depth),
        out_shape=(out, out),
        in_specs=[index, index, whole, anywhere, anywhere],
        out_specs=(whole, whole),
        scratch_shapes=[
            pltpu.VMEM((depth, width), jnp.float32),
            pltpu.VMEM((depth, width), jnp.float32),
            pltpu.VMEM((rows, depth), jnp.float32),
            pltpu.VMEM((rows, depth), jnp.float32),
            pltpu.SemaphoreType.DMA((2,)),
        ],
        compiler_params=pltpu.CompilerParams(vmem_limit_bytes=SMALL_LIMIT),
        cost_estimate=pl.CostEstimate(flops=16 * rows * inner * width, bytes_accessed=24 << 20, transcendentals=0),
        name="child",
    )(own_at, other_at, random, own, other)


def front_kernel(depth, blocks, random, own, other, out):
    step = pl.program_id(0)
    count = depth // 128

    @pl.when(step == 0)
    def _():
        out[...] = jnp.zeros_like(out)

    rows = [random[pl.ds(pl.multiple_of(blocks[step * count + i] * 128, 128), 128), :] for i in range(count)]
    columns = jnp.concatenate(held_halves(jnp.concatenate(rows, axis=0)), axis=1)
    stacked = jnp.concatenate(held_halves(jnp.concatenate([own[...], other[...]], axis=0)), axis=0)
    out[...] += joined(jnp.dot(stacked, columns, preferred_element_type=jnp.float32))


def front_product(blocks, random, own, other, depth=4096):
    rows, inner = own.shape
    width = random.shape[1]
    block = pl.BlockSpec((rows, depth), lambda k, *_: (0, k))
    return pl.pallas_call(
        functools.partial(front_kernel, depth),
        out_shape=jax.ShapeDtypeStruct((2 * rows, width), jnp.float32),
        grid_spec=pltpu.PrefetchScalarGridSpec(
            num_scalar_prefetch=1,
            grid=(inner // depth,),
            in_specs=[pl.BlockSpec(random.shape, lambda k, *_: (0, 0), pipeline_mode=pl.Buffered(1)), block, block],
            out_specs=pl.BlockSpec((2 * rows, width), lambda k, *_: (0, 0)),
        ),
        compiler_params=pltpu.CompilerParams(vmem_limit_bytes=VMEM_LIMIT),
        cost_estimate=pl.CostEstimate(flops=16 * rows * inner * width, bytes_accessed=24 << 20, transcendentals=0),
        name="front",
    )(blocks, random, own, other)


def coordinates(block):
    front, grid = block >> 5, block & 31
    return grid & 3, (grid >> 2) & 3, (grid >> 4) * 2 + (front >> 1), front & 1


def far_cube(v, core):
    return ((v - 1 + core) & 3) >> 1


def held_block(block, here, core):
    *there, owner = coordinates(block)
    far = near = 0
    for i, (v, m) in enumerate(zip(there, here)):
        v = (v - core) & 3
        far += ((v >> 1) ^ far_cube(m, core) ^ core) << i
        near += (v & 1) << i
    return (far * 8 + near) * 2 + (owner ^ core)


def shards(index_map, lengths, update_front, front_matrix, random):
    me = lax.axis_index("front") * 32 + lax.axis_index("grid")
    core = lax.axis_index("front") & 1
    width = random.shape[1] // 2
    own_rows = random.shape[0]
    grid = lax.axis_index("grid")
    here = (grid & 3, (grid >> 2) & 3, (grid >> 4) * 2 + (lax.axis_index("front") >> 1))
    sample_rows = update_front.shape[1]

    own_update, own_front = update_front[0], front_matrix
    left, right = random[:, :width], random[:, width:]
    kept = jnp.where(core == 0, left, right)
    given = jnp.where(core == 0, right, left)
    halved = jnp.concatenate([kept, swap_cores(given)], axis=0)
    near = spread(halved, NEAR)

    own_map = jnp.concatenate([index_map[0], jnp.broadcast_to(lengths, (128,))])
    other_map = swap_cores(own_map)
    _, _, given_update = lax.optimization_barrier((halved, other_map, own_update))
    other_update = swap_cores(given_update)

    maps = jnp.stack([own_map, other_map])
    live = maps[:, -1]
    maps = maps[:, :-128]
    at = held_block(maps >> 7, here, core) * 128 + (maps & 127)
    own_at, other_at = at[0], at[1]
    first = grid * sample_rows
    rows = first + jnp.arange(sample_rows, dtype=jnp.int32)
    alive = rows[None, :] < live[:, None]
    blocks = held_block(jnp.arange(WHOLE_BLOCKS, dtype=jnp.int32), here, core)

    near, other_update, own_at, other_at, alive, blocks = lax.optimization_barrier(
        (near, other_update, own_at, other_at, alive, blocks)
    )
    gathered = spread(near.reshape(-1, width), FAR).reshape(-1, width)
    gathered, given_front, given_maps = lax.optimization_barrier((gathered, own_front, maps))
    next_maps = lax.ppermute(given_maps, AXES, LAYERS)
    other_front = swap_cores(given_front)

    samples = jnp.stack(child_products(own_at, other_at, gathered, own_update, other_update))
    samples = jnp.where(alive[:, :, None], samples, jnp.float32(0.0))
    samples, next_maps = lax.optimization_barrier((samples, next_maps))
    cube = spread(samples, NEAR).reshape(-1, width)
    _, blocks, maps, next_maps, here = lax.optimization_barrier((samples, blocks, maps, next_maps, here))
    front = front_product(blocks, gathered, own_front, other_front)

    layers = jnp.concatenate([maps, next_maps]).reshape(-1, sample_rows)
    wanted = lax.dynamic_index_in_dim(jnp.asarray(MAP_ROWS), me, 0, keepdims=False)
    targets = layers.at[wanted].get(mode="promise_in_bounds")
    *there, owner = coordinates(targets >> 7)
    ours = functools.reduce(jnp.logical_and, [far_cube(v, core) == far_cube(m, core) for v, m in zip(there, here)])
    member = sum(((v - 1 + core) & 1) << i for i, v in enumerate(there))
    slots = jnp.where(ours, (member * 2 + (owner ^ core)) * own_rows + (targets & (own_rows - 1)), -1)
    slots = slots.reshape(-1)

    cube, front = lax.optimization_barrier((cube, front))
    chosen = (jnp.arange(16 * own_rows, dtype=jnp.int32)[:, None] == slots[None, :]).astype(jnp.bfloat16)
    terms = jnp.dot(chosen, jnp.concatenate(halves(cube), axis=1), preferred_element_type=jnp.float32)
    terms = terms[:, :width] + terms[:, width:]
    parts = lax.all_to_all(terms.reshape(8, 2 * own_rows, width), AXES, 0, 0, tiled=True, axis_index_groups=FAR)
    total = front + jnp.sum(parts, axis=0)
    mine_half, other_half = total[:own_rows], swap_cores(total[own_rows:])
    return jnp.where(
        core == 0,
        jnp.concatenate([mine_half, other_half], axis=1),
        jnp.concatenate([other_half, mine_half], axis=1),
    )


VMEM_LIMIT = 48 << 20
SMALL_LIMIT = 32 << 20
WHOLE_BLOCKS = len(PLACES)


def solution(mesh):
    placed = (
        P("front", None),
        P("front"),
        P("front", "grid", None),
        P(("front", "grid"), None),
        P(("front", "grid"), None),
    )
    return jax.shard_map(
        shards, mesh=mesh, in_specs=placed, out_specs=P(("front", "grid"), None), check_vma=False
    )
```

```python
import functools

import jax
import jax.numpy as jnp
import numpy as np
from jax import lax
from jax.experimental import pallas as pl
from jax.experimental.pallas import tpu as pltpu
from jax.sharding import PartitionSpec as P

AXES = ("front", "grid")
SIDE = 4


def places():
    return [
        (x, y, z_hi * 2 + z_lo, core)
        for z_lo in range(2)
        for core in range(2)
        for z_hi in range(2)
        for y in range(SIDE)
        for x in range(SIDE)
    ]


PLACES = places()
DEVICE = {place: i for i, place in enumerate(PLACES)}
BITS = [(z, y, x) for z in range(2) for y in range(2) for x in range(2)]


def near_groups():
    groups = []
    for core in range(2):
        for cube in BITS:
            groups.append(
                [
                    DEVICE[tuple((2 * c + b + core) % SIDE for c, b in zip(cube[::-1], bit[::-1])) + (core,)]
                    for bit in BITS
                ]
            )
    return groups


def far_groups():
    groups = []
    for core in range(2):
        for cube in BITS:
            groups.append(
                [
                    DEVICE[tuple((2 * c + b + 1 - core) % SIDE for c, b in zip(cube[::-1], bit[::-1])) + (core,)]
                    for bit in BITS
                ]
            )
    return groups


NEAR = near_groups()
FAR = far_groups()
CORES = [(i, DEVICE[(x, y, z, 1 - core)]) for i, (x, y, z, core) in enumerate(PLACES)]
LAYERS = [(i, DEVICE[(x, y, z ^ 1, core)]) for i, (x, y, z, core) in enumerate(PLACES)]


def map_rows():
    rows = np.zeros((len(PLACES), 16), np.int32)
    for group in NEAR:
        for d in group:
            for j, m in enumerate(group):
                x, y, z, _ = PLACES[m]
                for other in range(2):
                    layer = (z ^ PLACES[d][2]) & 1
                    rows[d, 2 * j + other] = (layer * 2 + other) * 32 + (z // 2) * 16 + y * 4 + x
    return rows


MAP_ROWS = map_rows()


def swap_cores(a):
    return lax.ppermute(a, AXES, CORES)


def spread(a, groups):
    copies = jnp.broadcast_to(a[None], (len(groups[0]), *a.shape))
    return lax.all_to_all(copies, AXES, 0, 0, tiled=True, axis_index_groups=groups)


def halves(a):
    high = lax.reduce_precision(a, 8, 7)
    return high.astype(jnp.bfloat16), (a - high).astype(jnp.bfloat16)


def held_halves(rows):
    high = rows.astype(jnp.bfloat16)
    low = (rows - high.astype(jnp.float32)).astype(jnp.bfloat16)
    return high, low


def joined(p):
    m, n = p.shape[0] // 2, p.shape[1] // 2
    return (p[:m, :n] + p[m:, :n]) + (p[:m, n:] + p[m:, n:])


def child_kernel(depth, own_at, other_at, random, own, other, own_out, other_out, even, odd, own_held, other_held, sems):
    chunks = own.shape[1] // depth
    place = lax.broadcasted_iota(jnp.int32, (8, 128), 0)

    def fetch(chunk, update, held, sem):
        columns = pl.ds(pl.multiple_of(chunk * depth, depth), depth)
        return pltpu.make_async_copy(update.at[:, columns], held, sem)

    def gather(at, chunk, rows):
        base = chunk * depth
        for j in range(0, depth, 8):
            tile = jnp.broadcast_to(random[pl.ds(at[base + j], 1), :], (8, 128))
            for t in range(1, 8):
                row = jnp.broadcast_to(random[pl.ds(at[base + j + t], 1), :], (8, 128))
                tile = jnp.where(place == t, row, tile)
            rows[j : j + 8, :] = tile

    def product(held, rows, out):
        stacked = jnp.concatenate(held_halves(held[...]), axis=0)
        columns = jnp.concatenate(held_halves(rows[...]), axis=1)
        out[...] += joined(jnp.dot(stacked, columns, preferred_element_type=jnp.float32))

    fetch(0, own, own_held, sems.at[0]).start()
    fetch(0, other, other_held, sems.at[1]).start()
    gather(own_at, 0, even)
    own_out[...] = jnp.zeros_like(own_out)
    other_out[...] = jnp.zeros_like(other_out)

    def step(i, carry):
        fetch(i, own, own_held, sems.at[0]).wait()
        gather(other_at, i, odd)
        product(own_held, even, own_out)

        @pl.when(i + 1 < chunks)
        def _():
            fetch(i + 1, own, own_held, sems.at[0]).start()

        fetch(i, other, other_held, sems.at[1]).wait()
        gather(own_at, jnp.minimum(i + 1, chunks - 1), even)
        product(other_held, odd, other_out)

        @pl.when(i + 1 < chunks)
        def _():
            fetch(i + 1, other, other_held, sems.at[1]).start()

        return carry

    lax.fori_loop(0, chunks, step, 0)


def child_products(own_at, other_at, random, own, other, depth=2048):
    rows, inner = own.shape
    width = random.shape[1]
    whole = pl.BlockSpec(memory_space=pltpu.VMEM)
    anywhere = pl.BlockSpec(memory_space=pl.ANY)
    index = pl.BlockSpec(memory_space=pltpu.SMEM)
    out = jax.ShapeDtypeStruct((rows, width), jnp.float32)
    return pl.pallas_call(
        functools.partial(child_kernel, depth),
        out_shape=(out, out),
        in_specs=[index, index, whole, anywhere, anywhere],
        out_specs=(whole, whole),
        scratch_shapes=[
            pltpu.VMEM((depth, width), jnp.float32),
            pltpu.VMEM((depth, width), jnp.float32),
            pltpu.VMEM((rows, depth), jnp.float32),
            pltpu.VMEM((rows, depth), jnp.float32),
            pltpu.SemaphoreType.DMA((2,)),
        ],
        compiler_params=pltpu.CompilerParams(vmem_limit_bytes=SMALL_LIMIT),
        cost_estimate=pl.CostEstimate(flops=16 * rows * inner * width, bytes_accessed=24 << 20, transcendentals=0),
        name="child",
    )(own_at, other_at, random, own, other)


def front_kernel(depth, blocks, random, own, other, out):
    step = pl.program_id(0)
    count = depth // 128

    @pl.when(step == 0)
    def _():
        out[...] = jnp.zeros_like(out)

    rows = [random[pl.ds(pl.multiple_of(blocks[step * count + i] * 128, 128), 128), :] for i in range(count)]
    columns = jnp.concatenate(held_halves(jnp.concatenate(rows, axis=0)), axis=1)
    stacked = jnp.concatenate(held_halves(jnp.concatenate([own[...], other[...]], axis=0)), axis=0)
    out[...] += joined(jnp.dot(stacked, columns, preferred_element_type=jnp.float32))


def front_product(blocks, random, own, other, depth=4096):
    rows, inner = own.shape
    width = random.shape[1]
    block = pl.BlockSpec((rows, depth), lambda k, *_: (0, k))
    return pl.pallas_call(
        functools.partial(front_kernel, depth),
        out_shape=jax.ShapeDtypeStruct((2 * rows, width), jnp.float32),
        grid_spec=pltpu.PrefetchScalarGridSpec(
            num_scalar_prefetch=1,
            grid=(inner // depth,),
            in_specs=[pl.BlockSpec(random.shape, lambda k, *_: (0, 0), pipeline_mode=pl.Buffered(1)), block, block],
            out_specs=pl.BlockSpec((2 * rows, width), lambda k, *_: (0, 0)),
        ),
        compiler_params=pltpu.CompilerParams(vmem_limit_bytes=VMEM_LIMIT),
        cost_estimate=pl.CostEstimate(flops=16 * rows * inner * width, bytes_accessed=24 << 20, transcendentals=0),
        name="front",
    )(blocks, random, own, other)


def coordinates(block):
    front, grid = block >> 5, block & 31
    return grid & 3, (grid >> 2) & 3, (grid >> 4) * 2 + (front >> 1), front & 1


def far_cube(v, core):
    return ((v - 1 + core) & 3) >> 1


def held_block(block, here, core):
    *there, owner = coordinates(block)
    far = near = 0
    for i, (v, m) in enumerate(zip(there, here)):
        v = (v - core) & 3
        far += ((v >> 1) ^ far_cube(m, core) ^ core) << i
        near += (v & 1) << i
    return (far * 8 + near) * 2 + (owner ^ core)


def shards(index_map, lengths, update_front, front_matrix, random):
    me = lax.axis_index("front") * 32 + lax.axis_index("grid")
    core = lax.axis_index("front") & 1
    width = random.shape[1] // 2
    own_rows = random.shape[0]
    grid = lax.axis_index("grid")
    here = (grid & 3, (grid >> 2) & 3, (grid >> 4) * 2 + (lax.axis_index("front") >> 1))
    sample_rows = update_front.shape[1]

    own_update, own_front = update_front[0], front_matrix
    left, right = random[:, :width], random[:, width:]
    kept = jnp.where(core == 0, left, right)
    given = jnp.where(core == 0, right, left)
    halved = jnp.concatenate([kept, swap_cores(given)], axis=0)
    own_map = jnp.concatenate([index_map[0], jnp.broadcast_to(lengths, (128,))])
    other_map = swap_cores(own_map)
    halved, other_map, given_update, here, grid, core, me = lax.optimization_barrier(
        (halved, other_map, own_update, here, grid, core, me)
    )
    other_update = swap_cores(given_update)
    near, own_map, other_map, here, grid, core, me = lax.optimization_barrier(
        (spread(halved, NEAR), own_map, other_map, here, grid, core, me)
    )

    maps = jnp.stack([own_map, other_map])
    live = maps[:, -1]
    maps = maps[:, :-128]
    at = held_block(maps >> 7, here, core) * 128 + (maps & 127)
    own_at, other_at = at[0], at[1]
    first = grid * sample_rows
    rows = first + jnp.arange(sample_rows, dtype=jnp.int32)
    alive = rows[None, :] < live[:, None]
    blocks = held_block(jnp.arange(WHOLE_BLOCKS, dtype=jnp.int32), here, core)

    near, other_update, own_at, other_at, alive, blocks = lax.optimization_barrier(
        (near, other_update, own_at, other_at, alive, blocks)
    )
    gathered = spread(near.reshape(-1, width), FAR).reshape(-1, width)
    gathered, given_front, given_maps = lax.optimization_barrier((gathered, own_front, maps))
    next_maps = lax.ppermute(given_maps, AXES, LAYERS)
    other_front = swap_cores(given_front)

    samples = jnp.stack(child_products(own_at, other_at, gathered, own_update, other_update))
    samples = jnp.where(alive[:, :, None], samples, jnp.float32(0.0))
    samples, next_maps = lax.optimization_barrier((samples, next_maps))
    cube = spread(samples, NEAR).reshape(-1, width)
    _, blocks, maps, next_maps, here = lax.optimization_barrier((samples, blocks, maps, next_maps, here))
    front = front_product(blocks, gathered, own_front, other_front)

    layers = jnp.concatenate([maps, next_maps]).reshape(-1, sample_rows)
    wanted = lax.dynamic_index_in_dim(jnp.asarray(MAP_ROWS), me, 0, keepdims=False)
    targets = layers.at[wanted].get(mode="promise_in_bounds")
    *there, owner = coordinates(targets >> 7)
    ours = functools.reduce(jnp.logical_and, [far_cube(v, core) == far_cube(m, core) for v, m in zip(there, here)])
    member = sum(((v - 1 + core) & 1) << i for i, v in enumerate(there))
    slots = jnp.where(ours, (member * 2 + (owner ^ core)) * own_rows + (targets & (own_rows - 1)), -1)
    slots = slots.reshape(-1)

    cube, front = lax.optimization_barrier((cube, front))
    chosen = (jnp.arange(16 * own_rows, dtype=jnp.int32)[:, None] == slots[None, :]).astype(jnp.bfloat16)
    terms = jnp.dot(chosen, jnp.concatenate(halves(cube), axis=1), preferred_element_type=jnp.float32)
    terms = terms[:, :width] + terms[:, width:]
    parts = lax.all_to_all(terms.reshape(8, 2 * own_rows, width), AXES, 0, 0, tiled=True, axis_index_groups=FAR)
    total = front + jnp.sum(parts, axis=0)
    mine_half, other_half = total[:own_rows], swap_cores(total[own_rows:])
    return jnp.where(
        core == 0,
        jnp.concatenate([mine_half, other_half], axis=1),
        jnp.concatenate([other_half, mine_half], axis=1),
    )


VMEM_LIMIT = 48 << 20
SMALL_LIMIT = 32 << 20
WHOLE_BLOCKS = len(PLACES)


def solution(mesh):
    placed = (
        P("front", None),
        P("front"),
        P("front", "grid", None),
        P(("front", "grid"), None),
        P(("front", "grid"), None),
    )
    return jax.shard_map(
        shards, mesh=mesh, in_specs=placed, out_specs=P(("front", "grid"), None), check_vma=False
    )
```

```python
import functools

import jax
import jax.numpy as jnp
import numpy as np
from jax import lax
from jax.experimental import pallas as pl
from jax.experimental.pallas import tpu as pltpu
from jax.sharding import PartitionSpec as P

AXES = ("front", "grid")
SIDE = 4


def places():
    return [
        (x, y, z_hi * 2 + z_lo, core)
        for z_lo in range(2)
        for core in range(2)
        for z_hi in range(2)
        for y in range(SIDE)
        for x in range(SIDE)
    ]


PLACES = places()
DEVICE = {place: i for i, place in enumerate(PLACES)}
BITS = [(z, y, x) for z in range(2) for y in range(2) for x in range(2)]


def near_groups():
    groups = []
    for core in range(2):
        for cube in BITS:
            groups.append(
                [
                    DEVICE[tuple((2 * c + b + core) % SIDE for c, b in zip(cube[::-1], bit[::-1])) + (core,)]
                    for bit in BITS
                ]
            )
    return groups


def far_groups():
    groups = []
    for core in range(2):
        for cube in BITS:
            groups.append(
                [
                    DEVICE[tuple((2 * c + b + 1 - core) % SIDE for c, b in zip(cube[::-1], bit[::-1])) + (core,)]
                    for bit in BITS
                ]
            )
    return groups


NEAR = near_groups()
FAR = far_groups()
CORES = [(i, DEVICE[(x, y, z, 1 - core)]) for i, (x, y, z, core) in enumerate(PLACES)]
LAYERS = [(i, DEVICE[(x, y, z ^ 1, core)]) for i, (x, y, z, core) in enumerate(PLACES)]


def map_rows():
    rows = np.zeros((len(PLACES), 16), np.int32)
    for group in NEAR:
        for d in group:
            for j, m in enumerate(group):
                x, y, z, _ = PLACES[m]
                for other in range(2):
                    layer = (z ^ PLACES[d][2]) & 1
                    rows[d, 2 * j + other] = (layer * 2 + other) * 32 + (z // 2) * 16 + y * 4 + x
    return rows


MAP_ROWS = map_rows()


def swap_cores(a):
    return lax.ppermute(a, AXES, CORES)


def spread(a, groups):
    copies = jnp.broadcast_to(a[None], (len(groups[0]), *a.shape))
    return lax.all_to_all(copies, AXES, 0, 0, tiled=True, axis_index_groups=groups)


def halves(a):
    high = lax.reduce_precision(a, 8, 7)
    return high.astype(jnp.bfloat16), (a - high).astype(jnp.bfloat16)


def held_halves(rows):
    high = rows.astype(jnp.bfloat16)
    low = (rows - high.astype(jnp.float32)).astype(jnp.bfloat16)
    return high, low


def joined(p):
    m, n = p.shape[0] // 2, p.shape[1] // 2
    return (p[:m, :n] + p[m:, :n]) + (p[:m, n:] + p[m:, n:])


def child_kernel(depth, own_at, other_at, random, own, other, own_out, other_out, even, odd, own_held, other_held, sems):
    chunks = own.shape[1] // depth
    place = lax.broadcasted_iota(jnp.int32, (8, 128), 0)

    def fetch(chunk, update, held, sem):
        columns = pl.ds(pl.multiple_of(chunk * depth, depth), depth)
        return pltpu.make_async_copy(update.at[:, columns], held, sem)

    def gather(at, chunk, rows):
        base = chunk * depth
        for j in range(0, depth, 8):
            tile = jnp.broadcast_to(random[pl.ds(at[base + j], 1), :], (8, 128))
            for t in range(1, 8):
                row = jnp.broadcast_to(random[pl.ds(at[base + j + t], 1), :], (8, 128))
                tile = jnp.where(place == t, row, tile)
            rows[j : j + 8, :] = tile

    def product(held, rows, out):
        stacked = jnp.concatenate(held_halves(held[...]), axis=0)
        columns = jnp.concatenate(held_halves(rows[...]), axis=1)
        out[...] += joined(jnp.dot(stacked, columns, preferred_element_type=jnp.float32))

    fetch(0, own, own_held, sems.at[0]).start()
    fetch(0, other, other_held, sems.at[1]).start()
    gather(own_at, 0, even)
    own_out[...] = jnp.zeros_like(own_out)
    other_out[...] = jnp.zeros_like(other_out)

    def step(i, carry):
        fetch(i, own, own_held, sems.at[0]).wait()
        gather(other_at, i, odd)
        product(own_held, even, own_out)
        fetch(i + 1, own, own_held, sems.at[0]).start()
        fetch(i, other, other_held, sems.at[1]).wait()
        gather(own_at, i + 1, even)
        product(other_held, odd, other_out)
        fetch(i + 1, other, other_held, sems.at[1]).start()
        return carry

    lax.fori_loop(0, chunks - 1, step, 0)
    fetch(chunks - 1, own, own_held, sems.at[0]).wait()
    gather(other_at, chunks - 1, odd)
    product(own_held, even, own_out)
    fetch(chunks - 1, other, other_held, sems.at[1]).wait()
    product(other_held, odd, other_out)


def child_products(own_at, other_at, random, own, other, depth=2048):
    rows, inner = own.shape
    width = random.shape[1]
    whole = pl.BlockSpec(memory_space=pltpu.VMEM)
    anywhere = pl.BlockSpec(memory_space=pl.ANY)
    index = pl.BlockSpec(memory_space=pltpu.SMEM)
    out = jax.ShapeDtypeStruct((rows, width), jnp.float32)
    return pl.pallas_call(
        functools.partial(child_kernel, depth),
        out_shape=(out, out),
        in_specs=[index, index, whole, anywhere, anywhere],
        out_specs=(whole, whole),
        scratch_shapes=[
            pltpu.VMEM((depth, width), jnp.float32),
            pltpu.VMEM((depth, width), jnp.float32),
            pltpu.VMEM((rows, depth), jnp.float32),
            pltpu.VMEM((rows, depth), jnp.float32),
            pltpu.SemaphoreType.DMA((2,)),
        ],
        compiler_params=pltpu.CompilerParams(vmem_limit_bytes=SMALL_LIMIT),
        cost_estimate=pl.CostEstimate(flops=16 * rows * inner * width, bytes_accessed=24 << 20, transcendentals=0),
        name="child",
    )(own_at, other_at, random, own, other)


def front_kernel(depth, blocks, random, own, other, out):
    step = pl.program_id(0)
    count = depth // 128

    @pl.when(step == 0)
    def _():
        out[...] = jnp.zeros_like(out)

    rows = [random[pl.ds(pl.multiple_of(blocks[step * count + i] * 128, 128), 128), :] for i in range(count)]
    columns = jnp.concatenate(held_halves(jnp.concatenate(rows, axis=0)), axis=1)
    stacked = jnp.concatenate(held_halves(jnp.concatenate([own[...], other[...]], axis=0)), axis=0)
    out[...] += joined(jnp.dot(stacked, columns, preferred_element_type=jnp.float32))


def front_product(blocks, random, own, other, depth=4096):
    rows, inner = own.shape
    width = random.shape[1]
    block = pl.BlockSpec((rows, depth), lambda k, *_: (0, k))
    return pl.pallas_call(
        functools.partial(front_kernel, depth),
        out_shape=jax.ShapeDtypeStruct((2 * rows, width), jnp.float32),
        grid_spec=pltpu.PrefetchScalarGridSpec(
            num_scalar_prefetch=1,
            grid=(inner // depth,),
            in_specs=[pl.BlockSpec(random.shape, lambda k, *_: (0, 0), pipeline_mode=pl.Buffered(1)), block, block],
            out_specs=pl.BlockSpec((2 * rows, width), lambda k, *_: (0, 0)),
        ),
        compiler_params=pltpu.CompilerParams(vmem_limit_bytes=VMEM_LIMIT),
        cost_estimate=pl.CostEstimate(flops=16 * rows * inner * width, bytes_accessed=24 << 20, transcendentals=0),
        name="front",
    )(blocks, random, own, other)


def coordinates(block):
    front, grid = block >> 5, block & 31
    return grid & 3, (grid >> 2) & 3, (grid >> 4) * 2 + (front >> 1), front & 1


def far_cube(v, core):
    return ((v - 1 + core) & 3) >> 1


def held_block(block, here, core):
    *there, owner = coordinates(block)
    far = near = 0
    for i, (v, m) in enumerate(zip(there, here)):
        v = (v - core) & 3
        far += ((v >> 1) ^ far_cube(m, core) ^ core) << i
        near += (v & 1) << i
    return (far * 8 + near) * 2 + (owner ^ core)


def shards(index_map, lengths, update_front, front_matrix, random):
    me = lax.axis_index("front") * 32 + lax.axis_index("grid")
    core = lax.axis_index("front") & 1
    width = random.shape[1] // 2
    own_rows = random.shape[0]
    grid = lax.axis_index("grid")
    here = (grid & 3, (grid >> 2) & 3, (grid >> 4) * 2 + (lax.axis_index("front") >> 1))
    sample_rows = update_front.shape[1]

    own_update, own_front = update_front[0], front_matrix
    left, right = random[:, :width], random[:, width:]
    kept = jnp.where(core == 0, left, right)
    given = jnp.where(core == 0, right, left)
    halved = jnp.concatenate([kept, swap_cores(given)], axis=0)
    own_map = jnp.concatenate([index_map[0], jnp.broadcast_to(lengths, (128,))])
    other_map = swap_cores(own_map)
    halved, other_map, given_update, here, grid, core, me = lax.optimization_barrier(
        (halved, other_map, own_update, here, grid, core, me)
    )
    other_update = swap_cores(given_update)
    near, own_map, other_map, here, grid, core, me = lax.optimization_barrier(
        (spread(halved, NEAR), own_map, other_map, here, grid, core, me)
    )

    maps = jnp.stack([own_map, other_map])
    live = maps[:, -1]
    maps = maps[:, :-128]
    at = held_block(maps >> 7, here, core) * 128 + (maps & 127)
    own_at, other_at = at[0], at[1]
    first = grid * sample_rows
    rows = first + jnp.arange(sample_rows, dtype=jnp.int32)
    alive = rows[None, :] < live[:, None]
    blocks = held_block(jnp.arange(WHOLE_BLOCKS, dtype=jnp.int32), here, core)

    near, other_update, own_at, other_at, alive, blocks = lax.optimization_barrier(
        (near, other_update, own_at, other_at, alive, blocks)
    )
    gathered = spread(near.reshape(-1, width), FAR).reshape(-1, width)
    gathered, given_front, given_maps = lax.optimization_barrier((gathered, own_front, maps))
    next_maps = lax.ppermute(given_maps, AXES, LAYERS)
    other_front = swap_cores(given_front)

    samples = jnp.stack(child_products(own_at, other_at, gathered, own_update, other_update))
    samples = jnp.where(alive[:, :, None], samples, jnp.float32(0.0))
    samples, next_maps = lax.optimization_barrier((samples, next_maps))
    cube = spread(samples, NEAR).reshape(-1, width)
    _, blocks, maps, next_maps, here = lax.optimization_barrier((samples, blocks, maps, next_maps, here))
    front = front_product(blocks, gathered, own_front, other_front)

    layers = jnp.concatenate([maps, next_maps]).reshape(-1, sample_rows)
    wanted = lax.dynamic_index_in_dim(jnp.asarray(MAP_ROWS), me, 0, keepdims=False)
    targets = layers.at[wanted].get(mode="promise_in_bounds")
    *there, owner = coordinates(targets >> 7)
    ours = functools.reduce(jnp.logical_and, [far_cube(v, core) == far_cube(m, core) for v, m in zip(there, here)])
    member = sum(((v - 1 + core) & 1) << i for i, v in enumerate(there))
    slots = jnp.where(ours, (member * 2 + (owner ^ core)) * own_rows + (targets & (own_rows - 1)), -1)
    slots = slots.reshape(-1)

    cube, front = lax.optimization_barrier((cube, front))
    chosen = (jnp.arange(16 * own_rows, dtype=jnp.int32)[:, None] == slots[None, :]).astype(jnp.bfloat16)
    terms = jnp.dot(chosen, jnp.concatenate(halves(cube), axis=1), preferred_element_type=jnp.float32)
    terms = terms[:, :width] + terms[:, width:]
    parts = lax.all_to_all(terms.reshape(8, 2 * own_rows, width), AXES, 0, 0, tiled=True, axis_index_groups=FAR)
    total = front + jnp.sum(parts, axis=0)
    mine_half, other_half = total[:own_rows], swap_cores(total[own_rows:])
    return jnp.where(
        core == 0,
        jnp.concatenate([mine_half, other_half], axis=1),
        jnp.concatenate([other_half, mine_half], axis=1),
    )


VMEM_LIMIT = 48 << 20
SMALL_LIMIT = 32 << 20
WHOLE_BLOCKS = len(PLACES)


def solution(mesh):
    placed = (
        P("front", None),
        P("front"),
        P("front", "grid", None),
        P(("front", "grid"), None),
        P(("front", "grid"), None),
    )
    return jax.shard_map(
        shards, mesh=mesh, in_specs=placed, out_specs=P(("front", "grid"), None), check_vma=False
    )
```
